512 devices in a mesh: dp: 8 (over x_hi, y), fsdp: 16 (over z), tensor: 4 (over x_lo, core).
Axes of the slice: x: 4 (x_hi: 2, x_lo: 2; x = x_hi * 2 + x_lo), y: 4, z: 16, core: 2. Of those that a mesh axis runs over, the one named last changes fastest.
Arguments:
- grad_part: bfloat16 [8, 16, 2048, 1024], P('dp', 'fsdp', None, 'tensor'), may hold values from -900 to 900
- gain_grad_part: bfloat16 [8, 16, 4, 2048], P('dp', 'fsdp', 'tensor'), may hold values from -840 to 840
- master: float32 [2048, 1024], P('fsdp', 'tensor'), may hold values from -0.005 to 0.005
- moment_one: float32 [2048, 1024], P('fsdp', 'tensor'), may hold values from -2.4 to 2.4
- moment_two: float32 [2048, 1024], P('fsdp', 'tensor'), may hold values from 0.05 to 1.5
- teacher: float32 [2048, 1024], P('fsdp', 'tensor'), may hold values from -0.005 to 0.005
- gain_master: float32 [2048], P('fsdp'), may hold values from -0.008 to 0.008
- gain_moment_one: float32 [2048], P('fsdp'), may hold values from -18 to 18
- gain_moment_two: float32 [2048], P('fsdp'), may hold values from 2 to 32
- gain_teacher: float32 [2048], P('fsdp'), may hold values from -0.008 to 0.008
Outputs:
- weights: bfloat16 [2048, 1024], P(None, 'tensor')
- gain_weights: bfloat16 [2048], replicated
- master_new: float32 [2048, 1024], P('fsdp', 'tensor')
- moment_one_new: float32 [2048, 1024], P('fsdp', 'tensor')
- moment_two_new: float32 [2048, 1024], P('fsdp', 'tensor')
- teacher_new: float32 [2048, 1024], P('fsdp', 'tensor')
- gain_master_new: float32 [2048], P('fsdp')
- gain_moment_one_new: float32 [2048], P('fsdp')
- gain_moment_two_new: float32 [2048], P('fsdp')
- gain_teacher_new: float32 [2048], P('fsdp')
The draws below stay inside these ranges and needn't reach their ends.
All inputs are finite; a program needn't handle non-finite values.
Results may differ from the reference program's by a relative error of at most 0.001.
Values may be sent and summed in bfloat16 or wider, within the bound.
No kernel may reach another device: no remote copies, remote signals or barrier semaphores. Data moves between devices by JAX's collectives and lax.ppermute only.
A program may use at most 64 MiB of HBM per device.

```python
import math
import jax
import jax.numpy as jnp
from jax import lax

D = 2048
HEADS = 8
HEAD = 128
STEP = 20
COLS = 1024
N_DP = 8
N_FSDP = 16
N_TENSOR = 4


def scale_profile(key, count):
    steady = jnp.arange(count, dtype=jnp.float32) / max(count - 1, 1)
    rising = jnp.exp(0.5 * math.log(3.0) * steady)
    spread = 10.0 ** jax.random.uniform(key, (count,), jnp.float32)
    return rising * spread


def block_factors(key):
    block_count = N_FSDP
    levels = -2.0 * jnp.arange(block_count, dtype=jnp.float32) / max(block_count - 1, 1)
    placing = jax.random.permutation(key, block_count)
    return jnp.repeat(jnp.power(10.0, levels[placing]), D // block_count)


def draw_grad_part(key, part):
    subkeys = jax.random.split(jax.random.fold_in(key, 11), 5)
    row_scale = scale_profile(subkeys[0], D) * block_factors(subkeys[4])
    col_scale = scale_profile(subkeys[1], HEADS * HEAD)
    full_shape = (N_DP, N_FSDP, D, HEADS * HEAD)
    noise = jax.random.normal(subkeys[3], full_shape, jnp.float32)
    noise = jnp.clip(noise, -6.0, 6.0)
    return (0.5 * noise * row_scale[:, None] * col_scale[None, :]).astype(jnp.bfloat16)


def draw_gain_grad_part(key, part):
    subkeys = jax.random.split(jax.random.fold_in(key, 23), 3)
    row_scale = scale_profile(subkeys[0], D)
    full_shape = (N_DP, N_FSDP, N_TENSOR, D)
    noise = jax.random.normal(subkeys[2], full_shape, jnp.float32)
    noise = jnp.clip(noise, -6.0, 6.0)
    level = 0.5 * math.sqrt(HEADS * HEAD / N_TENSOR)
    return (level * noise * row_scale).astype(jnp.bfloat16)


def block_levels(stream_key, dims, cuts, low, high):
    def one(position, parts):
        steps = jax.random.uniform(jax.random.fold_in(jax.random.fold_in(stream_key, 6), position), (parts,), jnp.float32, low / len(cuts), high / len(cuts))
        return jnp.repeat(jnp.exp(steps), dims[position] // parts).reshape((-1,) + (1,) * (len(dims) - position - 1))

    gain = one(*cuts[0])
    for cut in cuts[1:]:
        gain = gain * one(*cut)
    return gain


def scatter_about(key, shape, width, reach, cuts=(), held_as=jnp.bfloat16):
    entries = jax.random.normal(key, shape, jnp.float32) * width
    if len(cuts) > 0:
        entries = block_levels(key, shape, cuts, -0.22, 0.18) * entries
    return jnp.clip(entries, min=-reach, max=reach).astype(held_as)


def setup_inputs(seed: int = 0) -> dict:
    streams_of = jax.random.split(jax.random.key(seed), 11)
    grad_part = draw_grad_part(jax.random.fold_in(streams_of[10], 71), 0)
    gain_grad_part = draw_gain_grad_part(jax.random.fold_in(streams_of[10], 71), 0)
    master = jnp.clip(jax.random.uniform(streams_of[2], (D, COLS), jnp.float32, -0.005, 0.005) * block_levels(streams_of[2], (D, COLS), ((0, 16), (1, 4)), -0.4, 0.0), -0.005, 0.005)
    moment_one = scatter_about(streams_of[3], (D, COLS), 0.4, 2.4, ((0, 16), (1, 4)), jnp.float32)
    moment_two = jnp.clip(jnp.exp(math.log(1.5) - 3.4011974 * jax.random.uniform(streams_of[4], (D, COLS), jnp.float32) ** block_levels(streams_of[4], (D, COLS), ((0, 16), (1, 4)), -0.2, 0.2)), 0.05, 1.5)
    teacher = jnp.clip(jax.random.uniform(streams_of[5], (D, COLS), jnp.float32, -0.005, 0.005) * block_levels(streams_of[5], (D, COLS), ((0, 16), (1, 4)), -0.4, 0.0), -0.005, 0.005)
    gain_master = jnp.clip(jax.random.uniform(streams_of[6], (D,), jnp.float32, -0.008, 0.008) * block_levels(streams_of[6], (D,), ((0, 16),), -0.4, 0.0), -0.008, 0.008)
    gain_moment_one = scatter_about(streams_of[7], (D,), 3.0, 18.0, ((0, 16),), jnp.float32)
    gain_moment_two = jnp.clip(jnp.exp(math.log(32.0) - 2.7725887 * jax.random.uniform(streams_of[8], (D,), jnp.float32) ** block_levels(streams_of[8], (D,), ((0, 16),), -0.2, 0.2)), 2.0, 32.0)
    gain_teacher = jnp.clip(jax.random.uniform(streams_of[9], (D,), jnp.float32, -0.008, 0.008) * block_levels(streams_of[9], (D,), ((0, 16),), -0.4, 0.0), -0.008, 0.008)
    return {"grad_part": grad_part, "gain_grad_part": gain_grad_part, "master": master, "moment_one": moment_one, "moment_two": moment_two, "teacher": teacher, "gain_master": gain_master, "gain_moment_one": gain_moment_one, "gain_moment_two": gain_moment_two, "gain_teacher": gain_teacher}


beta_one = 0.9
beta_two = 0.95
learn_rate = 0.001
teacher_keep = 0.996
clip_level = 2.0
tiny_epsilon = 1e-08

def adamw(parameter, first_moment, second_moment, gradient, clip_factor, weight_decay, shadow):
    scaled = gradient * clip_factor
    first_new = beta_one * first_moment + (1.0 - beta_one) * scaled
    second_new = beta_two * second_moment + (1.0 - beta_two) * scaled * scaled
    corr_one = 1.0 - beta_one ** STEP
    corr_two = 1.0 - beta_two ** STEP
    direction = first_new / corr_one / (jnp.sqrt(second_new / corr_two) + tiny_epsilon)
    parameter_new = parameter - learn_rate * (direction + weight_decay * parameter)
    shadow_new = teacher_keep * shadow + (1.0 - teacher_keep) * parameter_new
    return (parameter_new, first_new, second_new, shadow_new)

def reference(grad_part, gain_grad_part, master, moment_one, moment_two, teacher, gain_master, gain_moment_one, gain_moment_two, gain_teacher):

    def add_replica(running, replica_block):
        return (running + lax.optimization_barrier(jnp.sum(replica_block.astype(jnp.float32), axis=0)), None)
    gradient, _ = lax.scan(add_replica, jnp.zeros((D, HEADS * HEAD), jnp.float32), grad_part)
    gain_gradient = lax.optimization_barrier(jnp.sum(gain_grad_part.astype(jnp.float32), axis=(0, 1, 2)))
    squares = jnp.sum(gradient * gradient) + jnp.sum(gain_gradient * gain_gradient)
    clip_limit = clip_level * math.sqrt(D * HEADS * HEAD + D)
    clip_factor = clip_limit / (jnp.sqrt(squares) + 1e-06)
    matrix_state = adamw(master, moment_one, moment_two, gradient, clip_factor, 0.1, teacher)
    gain_state = adamw(gain_master, gain_moment_one, gain_moment_two, gain_gradient, clip_factor, 0.0, gain_teacher)
    return (matrix_state[0].astype(jnp.bfloat16), gain_state[0].astype(jnp.bfloat16), matrix_state[0], matrix_state[1], matrix_state[2], matrix_state[3], gain_state[0], gain_state[1], gain_state[2], gain_state[3])
```

```python
import math

import jax
import jax.numpy as jnp
from jax import lax
from jax.sharding import PartitionSpec as P

D = 2048
HEADS = 8
HEAD = 128
STEP = 20


beta_one = 0.9
beta_two = 0.95
learn_rate = 0.001
teacher_keep = 0.996
clip_level = 2.0
tiny_epsilon = 1e-08


def adamw(parameter, first_moment, second_moment, gradient, clip_factor, weight_decay, shadow):
    scaled = gradient * clip_factor
    first_new = beta_one * first_moment + (1.0 - beta_one) * scaled
    second_new = beta_two * second_moment + (1.0 - beta_two) * scaled * scaled
    corr_one = 1.0 - beta_one**STEP
    corr_two = 1.0 - beta_two**STEP
    direction = first_new / corr_one / (jnp.sqrt(second_new / corr_two) + tiny_epsilon)
    parameter_new = parameter - learn_rate * (direction + weight_decay * parameter)
    shadow_new = teacher_keep * shadow + (1.0 - teacher_keep) * parameter_new
    return (parameter_new, first_new, second_new, shadow_new)


def exchange(blocks, axis):
    return lax.all_to_all(blocks, axis, 0, 0, tiled=True)


def to_all(block, count, axis):
    return exchange(jnp.broadcast_to(block[None], (count, *block.shape)), axis)


def shards(
    grad_part,
    gain_grad_part,
    master,
    moment_one,
    moment_two,
    teacher,
    gain_master,
    gain_moment_one,
    gain_moment_two,
    gain_teacher,
):
    n_dp, n_fsdp = lax.axis_size("dp"), lax.axis_size("fsdp")
    rows, cols = grad_part.shape[2:]
    piece = rows // (n_dp * n_fsdp)
    lines = piece * cols // 128

    with jax.named_scope("sum_dp"):
        pieces = grad_part.reshape(n_fsdp, n_dp, piece, cols).transpose(1, 0, 2, 3)
        pieces = pieces.reshape(n_dp, n_fsdp * piece, cols)
        gain_pieces = gain_grad_part.reshape(n_fsdp, n_dp, piece).transpose(1, 0, 2)
        gain_pieces = gain_pieces.reshape(n_dp, 1, n_fsdp * piece)
        gain_pieces = jnp.pad(gain_pieces, ((0, 0), (0, 7), (0, 0)))
        got = exchange(jnp.concatenate([pieces, gain_pieces], axis=1), "dp")
        summed = jnp.sum(got.astype(jnp.float32), axis=0)
    with jax.named_scope("sum_fsdp"):
        part = summed[: n_fsdp * piece].reshape(n_fsdp, lines, 128)
        gain_part = summed[n_fsdp * piece].reshape(n_fsdp, 1, piece)
        gain_part = jnp.pad(gain_part, ((0, 0), (0, 7), (0, 128 - piece)))
        got = exchange(jnp.concatenate([part, gain_part], axis=1), "fsdp")
        summed = jnp.sum(got, axis=0)
        own, own_gain = summed[:lines], summed[lines]
    with jax.named_scope("sum_tensor"):
        own_squares = jnp.sum(own * own)
        lane = lax.iota(jnp.int32, 128)
        total = lax.psum(jnp.where(lane == piece, own_squares, own_gain), "tensor")
        gain_piece = jnp.where(lane < piece, total, 0.0)
        squares = total[piece] + jnp.sum(gain_piece * gain_piece)
        line = jnp.where(lane == piece, squares, gain_piece)
    with jax.named_scope("share_dp"):
        block = jnp.concatenate([own, jnp.pad(line[None], ((0, 7), (0, 0)))], axis=0)
        got = to_all(block, n_dp, "dp")
        owned_rows = got[:, :lines].reshape(n_dp * piece, cols)
        owned_gain = got[:, lines, :piece].reshape(n_dp * piece)
        squares = jnp.sum(got[:, lines, piece])
    with jax.named_scope("squares_fsdp"):
        got = to_all(jnp.full((1, 128), squares), n_fsdp, "fsdp")
        total_squares = jnp.sum(got[:, 0, 0])
    clip_limit = clip_level * math.sqrt(D * HEADS * HEAD + D)
    clip_factor = clip_limit / (jnp.sqrt(total_squares) + 1e-06)
    matrix_state = adamw(master, moment_one, moment_two, owned_rows, clip_factor, 0.1, teacher)
    gain_state = adamw(
        gain_master, gain_moment_one, gain_moment_two, owned_gain, clip_factor, 0.0, gain_teacher
    )
    with jax.named_scope("weights_fsdp"):
        mine = matrix_state[0].astype(jnp.bfloat16).reshape(n_dp, lines, 128)
        mine = lax.dynamic_index_in_dim(mine, lax.axis_index("dp"), 0, keepdims=False)
        gain_mine = jnp.pad(gain_state[0].astype(jnp.bfloat16)[None], ((0, 7), (0, 0)))
        got = to_all(jnp.concatenate([mine, gain_mine], axis=0), n_fsdp, "fsdp")
        gain_weights = got[:, lines].reshape(rows)
    with jax.named_scope("weights_dp"):
        got = to_all(got[:, :lines].reshape(n_fsdp * piece, cols), n_dp, "dp")
        weights = got.reshape(n_dp, n_fsdp, piece, cols).transpose(1, 0, 2, 3).reshape(rows, cols)
    return (
        weights,
        gain_weights,
        matrix_state[0],
        matrix_state[1],
        matrix_state[2],
        matrix_state[3],
        gain_state[0],
        gain_state[1],
        gain_state[2],
        gain_state[3],
    )


def solution(mesh):
    return jax.shard_map(
        shards,
        mesh=mesh,
        in_specs=(
            P("dp", "fsdp", None, "tensor"),
            P("dp", "fsdp", "tensor", None),
            P("fsdp", "tensor"),
            P("fsdp", "tensor"),
            P("fsdp", "tensor"),
            P("fsdp", "tensor"),
            P("fsdp"),
            P("fsdp"),
            P("fsdp"),
            P("fsdp"),
        ),
        out_specs=(
            P(None, "tensor"),
            P(),
            P("fsdp", "tensor"),
            P("fsdp", "tensor"),
            P("fsdp", "tensor"),
            P("fsdp", "tensor"),
            P("fsdp"),
            P("fsdp"),
            P("fsdp"),
            P("fsdp"),
        ),
        check_vma=False,
    )
```

```python
import math

import jax
import jax.numpy as jnp
from jax import lax
from jax.sharding import PartitionSpec as P

D = 2048
HEADS = 8
HEAD = 128
STEP = 20


beta_one = 0.9
beta_two = 0.95
learn_rate = 0.001
teacher_keep = 0.996
clip_level = 2.0
tiny_epsilon = 1e-08


def adamw(parameter, first_moment, second_moment, gradient, clip_factor, weight_decay, shadow):
    scaled = gradient * clip_factor
    first_new = beta_one * first_moment + (1.0 - beta_one) * scaled
    second_new = beta_two * second_moment + (1.0 - beta_two) * scaled * scaled
    corr_one = 1.0 - beta_one**STEP
    corr_two = 1.0 - beta_two**STEP
    direction = first_new / corr_one / (jnp.sqrt(second_new / corr_two) + tiny_epsilon)
    parameter_new = parameter - learn_rate * (direction + weight_decay * parameter)
    shadow_new = teacher_keep * shadow + (1.0 - teacher_keep) * parameter_new
    return (parameter_new, first_new, second_new, shadow_new)


def exchange(blocks, axis):
    return lax.all_to_all(blocks, axis, 0, 0, tiled=True)


def to_all(block, count, axis):
    return exchange(jnp.broadcast_to(block[None], (count, *block.shape)), axis)


def shards(
    grad_part,
    gain_grad_part,
    master,
    moment_one,
    moment_two,
    teacher,
    gain_master,
    gain_moment_one,
    gain_moment_two,
    gain_teacher,
):
    n_dp, n_fsdp, n_tensor = (lax.axis_size(a) for a in ("dp", "fsdp", "tensor"))
    rows, cols = grad_part.shape[2:]
    block = rows // n_fsdp
    piece = block // n_dp
    lines = piece * cols // 128
    halves = cols // 128

    with jax.named_scope("sum_dp"):
        pieces = grad_part.reshape(n_fsdp, n_dp, piece, cols).transpose(1, 0, 2, 3)
        pieces = pieces.reshape(n_dp, n_fsdp * piece, cols)
        gain_rows = gain_grad_part.reshape(1, rows // cols, cols)
        gain_rows = jnp.broadcast_to(gain_rows, (n_dp, *gain_rows.shape[1:]))
        got = exchange(jnp.concatenate([pieces, gain_rows], axis=1), "dp")
        summed = jnp.sum(got.astype(jnp.float32), axis=0)
    with jax.named_scope("sum_fsdp"):
        part = summed[: n_fsdp * piece].reshape(n_fsdp, piece, cols)
        part = [part[:, :, 128 * h : 128 * (h + 1)] for h in range(halves)]
        gain_part = summed[n_fsdp * piece :].reshape(n_fsdp, 1, block)
        got = exchange(jnp.concatenate([*part, gain_part], axis=1), "fsdp")
        summed = jnp.sum(got, axis=0)
        own, own_gain = summed[:lines], summed[lines:]
        own_squares = jnp.sum(own * own, axis=0, keepdims=True)
    with jax.named_scope("squares_dp_tensor"):
        line = jnp.concatenate([own_gain, own_squares], axis=1)
        got = to_all(line, n_dp * n_tensor, ("dp", "tensor"))
        owned_gain = jnp.sum(got[:n_tensor, 0, :block], axis=0)
        squares = jnp.sum(got[:, 0, block:], axis=0) + owned_gain * owned_gain
    with jax.named_scope("squares_fsdp"):
        total_squares = jnp.sum(to_all(squares[None], n_fsdp, "fsdp"))
    clip_limit = clip_level * math.sqrt(D * HEADS * HEAD + D)
    clip_factor = clip_limit / (jnp.sqrt(total_squares) + 1e-06)
    gain_state = adamw(
        gain_master, gain_moment_one, gain_moment_two, owned_gain, clip_factor, 0.0, gain_teacher
    )
    with jax.named_scope("weights_fsdp"):
        own = jnp.concatenate([own[piece * h : piece * (h + 1)] for h in range(halves)], axis=1)
        high = lax.reduce_precision(own, 8, 7)
        low = lax.reduce_precision(own - high, 8, 7)
        first = lax.axis_index("dp") * piece
        state = [lax.dynamic_slice_in_dim(a, first, piece) for a in (master, moment_one, moment_two)]
        mine = adamw(*state, high + low, clip_factor, 0.1, jnp.float32(0))[0].astype(jnp.bfloat16)
        gain_mine = jnp.pad(gain_state[0].astype(jnp.bfloat16)[None], ((0, 0), (0, cols - block)))
        got = to_all(jnp.concatenate([mine, gain_mine], axis=0), n_fsdp, "fsdp")
        gain_weights = got[:, piece, :block].reshape(rows)
    with jax.named_scope("weights_dp"):
        mine = got[:, :piece].reshape(n_fsdp * piece, cols)
        terms = [t.astype(jnp.bfloat16) for t in (high, low)]
        got = to_all(jnp.concatenate([mine, *terms], axis=0), n_dp, "dp")
        weights = got[:, : n_fsdp * piece].reshape(n_dp, n_fsdp, piece, cols)
        weights = weights.transpose(1, 0, 2, 3).reshape(rows, cols)
        high, low = (
            got[:, (n_fsdp + i) * piece : (n_fsdp + i + 1) * piece].reshape(block, cols)
            for i in range(2)
        )
        owned_rows = high.astype(jnp.float32) + low.astype(jnp.float32)
    matrix_state = adamw(master, moment_one, moment_two, owned_rows, clip_factor, 0.1, teacher)
    return (
        weights,
        gain_weights,
        *matrix_state,
        *gain_state,
    )


def solution(mesh):
    return jax.shard_map(
        shards,
        mesh=mesh,
        in_specs=(
            P("dp", "fsdp", None, "tensor"),
            P("dp", "fsdp", "tensor", None),
            P("fsdp", "tensor"),
            P("fsdp", "tensor"),
            P("fsdp", "tensor"),
            P("fsdp", "tensor"),
            P("fsdp"),
            P("fsdp"),
            P("fsdp"),
            P("fsdp"),
        ),
        out_specs=(
            P(None, "tensor"),
            P(),
            P("fsdp", "tensor"),
            P("fsdp", "tensor"),
            P("fsdp", "tensor"),
            P("fsdp", "tensor"),
            P("fsdp"),
            P("fsdp"),
            P("fsdp"),
            P("fsdp"),
        ),
        check_vma=False,
    )
```

```python
import math

import jax
import jax.numpy as jnp
from jax import lax
from jax.sharding import PartitionSpec as P

D = 2048
HEADS = 8
HEAD = 128
STEP = 20


beta_one = 0.9
beta_two = 0.95
learn_rate = 0.001
teacher_keep = 0.996
clip_level = 2.0
tiny_epsilon = 1e-08


def adamw(parameter, first_moment, second_moment, gradient, clip_factor, weight_decay, shadow):
    scaled = gradient * clip_factor
    first_new = beta_one * first_moment + (1.0 - beta_one) * scaled
    second_new = beta_two * second_moment + (1.0 - beta_two) * scaled * scaled
    corr_one = 1.0 - beta_one**STEP
    corr_two = 1.0 - beta_two**STEP
    direction = first_new / corr_one / (jnp.sqrt(second_new / corr_two) + tiny_epsilon)
    parameter_new = parameter - learn_rate * (direction + weight_decay * parameter)
    shadow_new = teacher_keep * shadow + (1.0 - teacher_keep) * parameter_new
    return (parameter_new, first_new, second_new, shadow_new)


def exchange(blocks, axis):
    return lax.all_to_all(blocks, axis, 0, 0, tiled=True)


def to_all(block, count, axis):
    return exchange(jnp.broadcast_to(block[None], (count, *block.shape)), axis)


def shards(
    grad_part,
    gain_grad_part,
    master,
    moment_one,
    moment_two,
    teacher,
    gain_master,
    gain_moment_one,
    gain_moment_two,
    gain_teacher,
):
    n_dp, n_fsdp, n_tensor = (lax.axis_size(a) for a in ("dp", "fsdp", "tensor"))
    rows, cols = grad_part.shape[2:]
    block = rows // n_fsdp
    piece = block // n_dp
    lines = piece * cols // 128
    halves = cols // 128
    chunk = rows // n_dp
    ordered = lax.optimization_barrier

    with jax.named_scope("sum_dp"):
        pieces = grad_part.reshape(n_fsdp, n_dp, piece, cols).transpose(1, 0, 2, 3)
        pieces = pieces.reshape(n_dp, n_fsdp * piece, cols)
        pieces = jnp.concatenate([pieces, gain_grad_part.reshape(n_dp, chunk // cols, cols)], axis=1)
        owner, first = lax.axis_index("fsdp") * block, lax.axis_index("dp") * piece
        owner, first, pieces = ordered((owner, first, pieces))
        got = exchange(pieces, "dp")
        summed = jnp.sum(got.astype(jnp.float32), axis=0)
    with jax.named_scope("sum_fsdp"):
        part = summed[: n_fsdp * piece].reshape(n_fsdp, piece, cols)
        part = jnp.concatenate([part[:, :, 128 * h : 128 * (h + 1)] for h in range(halves)], axis=1)
        gain_part = summed[n_fsdp * piece :].reshape(1, chunk)
        part, gain_part = ordered((part, gain_part))
        own = jnp.sum(exchange(part, "fsdp"), axis=0)
        own, owner, first = ordered((own, owner, first))
        state = [lax.dynamic_slice_in_dim(a, first, piece) for a in (master, moment_one, moment_two)]
        own_squares = jnp.sum(own * own, axis=0, keepdims=True)
        own = jnp.concatenate([own[piece * h : piece * (h + 1)] for h in range(halves)], axis=1)
        high = lax.reduce_precision(own, 8, 7)
        low = lax.reduce_precision(own - high, 8, 7)
        own = high + low
        terms = jnp.concatenate([high.astype(jnp.bfloat16), low.astype(jnp.bfloat16)], axis=0)
    with jax.named_scope("squares_fsdp"):
        line = [a[None] for a in (gain_master, gain_moment_one, gain_moment_two)]
        line = jnp.concatenate([own_squares, gain_part, *line], axis=1)
        line, own, terms, state, owner = ordered((line, own, terms, state, owner))
        got = to_all(line, n_fsdp, "fsdp")
        gain_states = got[:, 0, 128 + chunk :].reshape(n_fsdp, 3, block)
        line = jnp.sum(got[:, :, : 128 + chunk], axis=0)
    with jax.named_scope("squares_dp_tensor"):
        line, gain_states = ordered((line, gain_states))
        got = to_all(line, n_dp * n_tensor, ("dp", "tensor"))
        gain = jnp.sum(got[:, 0, 128:].reshape(n_dp, n_tensor, chunk), axis=1)
        lane_squares = jnp.sum(got[:, :, :128], axis=0)
        for h in range(chunk // 128):
            half = gain[:, 128 * h : 128 * (h + 1)]
            lane_squares += jnp.sum(half * half, axis=0, keepdims=True)
        ones = jnp.ones((128, 128), jnp.float32)
        total_squares = jnp.dot(lane_squares, ones, precision=lax.Precision.HIGHEST)
    clip_limit = clip_level * math.sqrt(D * HEADS * HEAD + D)
    clip_factor = clip_limit / (jnp.sqrt(total_squares) + 1e-06)
    clip_row = jnp.concatenate([clip_factor] * halves, axis=1)
    zero = jnp.float32(0)
    with jax.named_scope("weights_fsdp"):
        mine = adamw(*state, own, clip_row, 0.1, zero)[0].astype(jnp.bfloat16)
        mine, gain = ordered((mine, gain))
        got = to_all(mine, n_fsdp, "fsdp")
    with jax.named_scope("weights_dp"):
        mine = jnp.concatenate([got.reshape(n_fsdp * piece, cols), terms], axis=0)
        mine, gain, gain_states, owner = ordered((mine, gain, gain_states, owner))
        got = to_all(mine, n_dp, "dp")
        weights = got[:, : n_fsdp * piece].reshape(n_dp, n_fsdp, piece, cols)
        weights = weights.transpose(1, 0, 2, 3).reshape(rows, cols)
        high, low = (
            got[:, (n_fsdp + i) * piece : (n_fsdp + i + 1) * piece].reshape(block, cols)
            for i in range(2)
        )
        owned_rows = high.astype(jnp.float32) + low.astype(jnp.float32)
    with jax.named_scope("gain"):
        gain = gain.reshape(n_fsdp, block)
        gain_states = [gain_states[:, i] for i in range(3)]
        gain_weights = adamw(*gain_states, gain, clip_factor, 0.0, zero)[0]
        gain_weights = gain_weights.astype(jnp.bfloat16).reshape(rows)
        owned_gain = lax.dynamic_slice_in_dim(gain.reshape(rows), owner, block)
        gain_state = adamw(
            gain_master, gain_moment_one, gain_moment_two, owned_gain, clip_factor[0], 0.0, gain_teacher
        )
    matrix_state = adamw(master, moment_one, moment_two, owned_rows, clip_row, 0.1, teacher)
    return (
        weights,
        gain_weights,
        *matrix_state,
        *gain_state,
    )


def solution(mesh):
    return jax.shard_map(
        shards,
        mesh=mesh,
        in_specs=(
            P("dp", "fsdp", None, "tensor"),
            P("dp", "fsdp", "tensor", None),
            P("fsdp", "tensor"),
            P("fsdp", "tensor"),
            P("fsdp", "tensor"),
            P("fsdp", "tensor"),
            P("fsdp"),
            P("fsdp"),
            P("fsdp"),
            P("fsdp"),
        ),
        out_specs=(
            P(None, "tensor"),
            P(),
            P("fsdp", "tensor"),
            P("fsdp", "tensor"),
            P("fsdp", "tensor"),
            P("fsdp", "tensor"),
            P("fsdp"),
            P("fsdp"),
            P("fsdp"),
            P("fsdp"),
        ),
        check_vma=False,
    )
```

```python
import math

import jax
import jax.numpy as jnp
from jax import lax
from jax.experimental import pallas as pl
from jax.experimental.pallas import tpu as pltpu
from jax.sharding import PartitionSpec as P

D = 2048
HEADS = 8
HEAD = 128
STEP = 20


beta_one = 0.9
beta_two = 0.95
learn_rate = 0.001
teacher_keep = 0.996
clip_level = 2.0
tiny_epsilon = 1e-08


def adamw(parameter, first_moment, second_moment, gradient, clip_factor, weight_decay, shadow):
    scaled = gradient * clip_factor
    first_new = beta_one * first_moment + (1.0 - beta_one) * scaled
    second_new = beta_two * second_moment + (1.0 - beta_two) * scaled * scaled
    corr_one = 1.0 - beta_one**STEP
    corr_two = 1.0 - beta_two**STEP
    direction = first_new / corr_one / (jnp.sqrt(second_new / corr_two) + tiny_epsilon)
    parameter_new = parameter - learn_rate * (direction + weight_decay * parameter)
    shadow_new = teacher_keep * shadow + (1.0 - teacher_keep) * parameter_new
    return (parameter_new, first_new, second_new, shadow_new)


def finish_kernel(*refs):
    got, clip = refs[:2]
    state, gain_weights, gain_state = refs[2:6], refs[6], refs[7]
    weights, gain_out, *outs = refs[8:18]
    terms, old, new, sems = refs[18], refs[19:23], refs[23:27], refs[27]
    n_dp, pieces, piece, cols = got.shape
    started = []

    def start(source, target):
        copy = pltpu.make_async_copy(source, target, sems.at[len(started)])
        copy.start()
        started.append(copy)

    start(got.at[:, pl.ds(pieces - 2, 2)], terms)
    for i in range(4):
        start(state[i], old[i])
    loads = len(started)
    for d in range(n_dp):
        start(got.at[d, pl.ds(0, pieces - 2)], weights.at[:, d])
    start(gain_weights, gain_out)
    for i in range(4):
        start(gain_state.at[pl.ds(i, 1)], outs[4 + i])
    for copy in started[:loads]:
        copy.wait()
    rows = terms[:, 0].astype(jnp.float32) + terms[:, 1].astype(jnp.float32)
    rows = rows.reshape(n_dp * piece, cols)
    values = adamw(*(ref[...] for ref in old[:3]), rows, clip[...], 0.1, old[3][...])
    for i in range(4):
        new[i][...] = values[i]
        start(new[i], outs[i])
    for copy in started[loads:]:
        copy.wait()


def finish(got, clip, state, gain_weights, gain_state):
    n_dp, pieces, piece, cols = got.shape
    owned = jax.ShapeDtypeStruct(state[0].shape, jnp.float32)
    gain = jax.ShapeDtypeStruct((1, gain_state.shape[1]), jnp.float32)
    anywhere = pl.BlockSpec(memory_space=pl.ANY)
    return pl.pallas_call(
        finish_kernel,
        out_shape=[
            jax.ShapeDtypeStruct((pieces - 2, n_dp, piece, cols), jnp.bfloat16),
            jax.ShapeDtypeStruct(gain_weights.shape, jnp.bfloat16),
            *[owned] * 4,
            *[gain] * 4,
        ],
        in_specs=[anywhere, pl.BlockSpec(memory_space=pltpu.VMEM)] + [anywhere] * 6,
        out_specs=[anywhere] * 10,
        scratch_shapes=[
            pltpu.VMEM((n_dp, 2, piece, cols), jnp.bfloat16),
            *[pltpu.VMEM(owned.shape, jnp.float32)] * 8,
            pltpu.SemaphoreType.DMA((14 + n_dp,)),
        ],
        compiler_params=pltpu.CompilerParams(vmem_limit_bytes=4 << 20),
        cost_estimate=pl.CostEstimate(flops=40 * 128 * 256, bytes_accessed=3 << 20, transcendentals=0),
    )(got, clip, *state, gain_weights, gain_state)


def exchange(blocks, axis):
    return lax.all_to_all(blocks, axis, 0, 0, tiled=True)


def to_all(block, count, axis):
    return exchange(jnp.broadcast_to(block[None], (count, *block.shape)), axis)


def shards(
    grad_part,
    gain_grad_part,
    master,
    moment_one,
    moment_two,
    teacher,
    gain_master,
    gain_moment_one,
    gain_moment_two,
    gain_teacher,
):
    n_dp, n_fsdp, n_tensor = (lax.axis_size(a) for a in ("dp", "fsdp", "tensor"))
    rows, cols = grad_part.shape[2:]
    block = rows // n_fsdp
    piece = block // n_dp
    lines = piece * cols // 128
    halves = cols // 128
    ordered = lax.optimization_barrier

    with jax.named_scope("sum_dp"):
        pieces = grad_part.reshape(n_fsdp, n_dp, piece, cols).transpose(1, 0, 2, 3)
        pieces = pieces.reshape(n_dp, n_fsdp * piece, cols)
        gain_rows = gain_grad_part.reshape(1, rows // cols, cols)
        gain_rows = jnp.broadcast_to(gain_rows, (n_dp, *gain_rows.shape[1:]))
        pieces = jnp.concatenate([pieces, gain_rows], axis=1)
        first, pieces = ordered((lax.axis_index("dp") * piece, pieces))
        got = exchange(pieces, "dp")
        summed = jnp.sum(got.astype(jnp.float32), axis=0)
    with jax.named_scope("sum_fsdp"):
        part = summed[: n_fsdp * piece].reshape(n_fsdp, piece, cols)
        part = jnp.concatenate([part[:, :, 128 * h : 128 * (h + 1)] for h in range(halves)], axis=1)
        gain_part = summed[n_fsdp * piece :].reshape(n_fsdp, 1, block)
        part = jnp.concatenate([part.reshape(n_fsdp, 1, lines * 128), gain_part], axis=2)
        summed = jnp.sum(exchange(part, "fsdp"), axis=0)
        summed, first = ordered((summed, first))
        own, own_gain = summed[:, : lines * 128].reshape(lines, 128), summed[:, lines * 128 :]
        state = [lax.dynamic_slice_in_dim(a, first, piece) for a in (master, moment_one, moment_two)]
        own_squares = jnp.sum(own * own, axis=0, keepdims=True)
        own = jnp.concatenate([own[piece * h : piece * (h + 1)] for h in range(halves)], axis=1)
        high = lax.reduce_precision(own, 8, 7)
        low = lax.reduce_precision(own - high, 8, 7)
        own = high + low
        terms = jnp.concatenate([high.astype(jnp.bfloat16), low.astype(jnp.bfloat16)], axis=0)
    with jax.named_scope("squares_dp_tensor"):
        line = jnp.concatenate([own_gain, own_squares], axis=1)
        line, own, terms, state = ordered((line, own, terms, state))
        got = to_all(line, n_dp * n_tensor, ("dp", "tensor"))
        owned_gain = jnp.sum(got[:n_tensor, :, :block], axis=0)
        squares = jnp.sum(got[:, :, block:], axis=0) + owned_gain * owned_gain
    with jax.named_scope("squares_fsdp"):
        line = [a[None] for a in (gain_master, gain_moment_one, gain_moment_two)]
        line = jnp.concatenate([squares, owned_gain, *line], axis=1)
        line, owned_gain = ordered((line, owned_gain))
        got = to_all(line, n_fsdp, "fsdp")
        lane_squares = jnp.sum(got[:, :, :block], axis=0)
        gain, *gain_states = [got[:, 0, block * i : block * (i + 1)] for i in range(1, 5)]
        ones = jnp.ones((128, 128), jnp.float32)
        total_squares = jnp.dot(lane_squares, ones, precision=lax.Precision.HIGHEST)
    clip_limit = clip_level * math.sqrt(D * HEADS * HEAD + D)
    clip_factor = clip_limit / (jnp.sqrt(total_squares) + 1e-06)
    clip_row = jnp.concatenate([clip_factor] * halves, axis=1)
    zero = jnp.float32(0)
    with jax.named_scope("gain"):
        gain_weights = adamw(*gain_states, gain, clip_factor, 0.0, zero)[0].astype(jnp.bfloat16)
        gain_state = (gain_master, gain_moment_one, gain_moment_two)
        gain_state = [a[None] for a in gain_state]
        gain_state = adamw(*gain_state, owned_gain, clip_factor, 0.0, gain_teacher[None])
        gain_state = jnp.concatenate(gain_state, axis=0)
    with jax.named_scope("weights_fsdp"):
        mine = adamw(*state, own, clip_row, 0.1, zero)[0].astype(jnp.bfloat16)
        mine, gain_weights, gain_state = ordered((mine, gain_weights, gain_state))
        got = to_all(mine, n_fsdp, "fsdp")
    with jax.named_scope("weights_dp"):
        mine = jnp.concatenate([got.reshape(n_fsdp * piece, cols), terms], axis=0)
        got = to_all(mine, n_dp, "dp")
        got = got.reshape(n_dp, n_fsdp + 2, piece, cols)
        state = (master, moment_one, moment_two, teacher)
        weights, gain_weights, *states = finish(got, clip_row, state, gain_weights, gain_state)
        matrix_state, gain_state = states[:4], [a.reshape(block) for a in states[4:]]
    return (
        weights.reshape(rows, cols),
        gain_weights.reshape(rows),
        *matrix_state,
        *gain_state,
    )


def solution(mesh):
    return jax.shard_map(
        shards,
        mesh=mesh,
        in_specs=(
            P("dp", "fsdp", None, "tensor"),
            P("dp", "fsdp", "tensor", None),
            P("fsdp", "tensor"),
            P("fsdp", "tensor"),
            P("fsdp", "tensor"),
            P("fsdp", "tensor"),
            P("fsdp"),
            P("fsdp"),
            P("fsdp"),
            P("fsdp"),
        ),
        out_specs=(
            P(None, "tensor"),
            P(),
            P("fsdp", "tensor"),
            P("fsdp", "tensor"),
            P("fsdp", "tensor"),
            P("fsdp", "tensor"),
            P("fsdp"),
            P("fsdp"),
            P("fsdp"),
            P("fsdp"),
        ),
        check_vma=False,
    )
```

```python
import math

import jax
import jax.numpy as jnp
from jax import lax
from jax.experimental import pallas as pl
from jax.experimental.pallas import tpu as pltpu
from jax.sharding import PartitionSpec as P

D = 2048
HEADS = 8
HEAD = 128
STEP = 20


beta_one = 0.9
beta_two = 0.95
learn_rate = 0.001
teacher_keep = 0.996
clip_level = 2.0
tiny_epsilon = 1e-08


def adamw(parameter, first_moment, second_moment, gradient, clip_factor, weight_decay, shadow):
    scaled = gradient * clip_factor
    first_new = beta_one * first_moment + (1.0 - beta_one) * scaled
    second_new = beta_two * second_moment + (1.0 - beta_two) * scaled * scaled
    corr_one = 1.0 - beta_one**STEP
    corr_two = 1.0 - beta_two**STEP
    direction = first_new / corr_one / (jnp.sqrt(second_new / corr_two) + tiny_epsilon)
    parameter_new = parameter - learn_rate * (direction + weight_decay * parameter)
    shadow_new = teacher_keep * shadow + (1.0 - teacher_keep) * parameter_new
    return (parameter_new, first_new, second_new, shadow_new)


def finish_kernel(*refs):
    got, clip = refs[:2]
    state, gain_weights, gain_state = refs[2:6], refs[6], refs[7]
    weights, gain_out, *outs = refs[8:18]
    new, sems = refs[18:22], refs[22]
    n_dp, pieces, piece, cols = got.shape
    copies = []

    def start(source, target):
        copy = pltpu.make_async_copy(source, target, sems.at[len(copies)])
        copy.start()
        copies.append(copy)

    for d in range(n_dp):
        start(got.at[d, pl.ds(0, pieces - 2)], weights.at[:, d])
    rows = got[:, pieces - 2].astype(jnp.float32) + got[:, pieces - 1].astype(jnp.float32)
    rows = rows.reshape(n_dp * piece, cols)
    values = adamw(*(ref[...] for ref in state[:3]), rows, clip[...], 0.1, state[3][...])
    for i in range(4):
        new[i][...] = values[i]
        start(new[i], outs[i])
    start(gain_weights, gain_out)
    for i in range(4):
        start(gain_state.at[pl.ds(i, 1)], outs[4 + i])
    for copy in copies:
        copy.wait()


def finish(got, clip, state, gain_weights, gain_state):
    n_dp, pieces, piece, cols = got.shape
    owned = jax.ShapeDtypeStruct(state[0].shape, jnp.float32)
    gain = jax.ShapeDtypeStruct((1, gain_state.shape[1]), jnp.float32)
    anywhere = pl.BlockSpec(memory_space=pl.ANY)
    return pl.pallas_call(
        finish_kernel,
        out_shape=[
            jax.ShapeDtypeStruct((pieces - 2, n_dp, piece, cols), jnp.bfloat16),
            jax.ShapeDtypeStruct(gain_weights.shape, jnp.bfloat16),
            *[owned] * 4,
            *[gain] * 4,
        ],
        in_specs=[pl.BlockSpec(memory_space=pltpu.VMEM)] * 8,
        out_specs=[anywhere] * 10,
        scratch_shapes=[
            *[pltpu.VMEM(owned.shape, jnp.float32)] * 4,
            pltpu.SemaphoreType.DMA((9 + n_dp,)),
        ],
        compiler_params=pltpu.CompilerParams(vmem_limit_bytes=8 << 20),
        cost_estimate=pl.CostEstimate(flops=40 * 128 * 256, bytes_accessed=3 << 20, transcendentals=0),
    )(got, clip, *state, gain_weights, gain_state)


def exchange(blocks, axis):
    return lax.all_to_all(blocks, axis, 0, 0, tiled=True)


def to_all(block, count, axis):
    return exchange(jnp.broadcast_to(block[None], (count, *block.shape)), axis)


def shards(
    grad_part,
    gain_grad_part,
    master,
    moment_one,
    moment_two,
    teacher,
    gain_master,
    gain_moment_one,
    gain_moment_two,
    gain_teacher,
):
    n_dp, n_fsdp, n_tensor = (lax.axis_size(a) for a in ("dp", "fsdp", "tensor"))
    rows, cols = grad_part.shape[2:]
    block = rows // n_fsdp
    piece = block // n_dp
    lines = piece * cols // 128
    halves = cols // 128
    ordered = lax.optimization_barrier

    with jax.named_scope("sum_dp"):
        pieces = grad_part.reshape(n_fsdp, n_dp, piece, cols).transpose(1, 0, 2, 3)
        pieces = pieces.reshape(n_dp, n_fsdp * piece, cols)
        pieces, gain_grad_part = ordered((pieces, gain_grad_part))
        gain_rows = gain_grad_part.reshape(1, rows // cols, cols)
        gain_rows = jnp.broadcast_to(gain_rows, (n_dp, *gain_rows.shape[1:]))
        pieces = jnp.concatenate([pieces, gain_rows], axis=1)
        first, pieces = ordered((lax.axis_index("dp") * piece, pieces))
        got = exchange(pieces, "dp")
        summed = jnp.sum(got.astype(jnp.float32), axis=0)
    with jax.named_scope("sum_fsdp"):
        part = summed[: n_fsdp * piece].reshape(n_fsdp, piece, cols)
        part = jnp.concatenate([part[:, :, 128 * h : 128 * (h + 1)] for h in range(halves)], axis=1)
        gain_part = summed[n_fsdp * piece :].reshape(n_fsdp, 1, block)
        part = jnp.concatenate([part.reshape(n_fsdp, 1, lines * 128), gain_part], axis=2)
        summed = jnp.sum(exchange(part, "fsdp"), axis=0)
        summed, first = ordered((summed, first))
        own, own_gain = summed[:, : lines * 128].reshape(lines, 128), summed[:, lines * 128 :]
        state = [lax.dynamic_slice_in_dim(a, first, piece) for a in (master, moment_one, moment_two)]
        own_squares = jnp.sum(own * own, axis=0, keepdims=True)
        own = jnp.concatenate([own[piece * h : piece * (h + 1)] for h in range(halves)], axis=1)
        high = lax.reduce_precision(own, 8, 7)
        low = lax.reduce_precision(own - high, 8, 7)
        own = high + low
        terms = jnp.concatenate([high.astype(jnp.bfloat16), low.astype(jnp.bfloat16)], axis=0)
    with jax.named_scope("squares_dp_tensor"):
        line = jnp.concatenate([own_gain, own_squares], axis=1)
        line, own, terms, state = ordered((line, own, terms, state))
        got = to_all(line, n_dp * n_tensor, ("dp", "tensor"))
        owned_gain = jnp.sum(got[:n_tensor, :, :block], axis=0)
        squares = jnp.sum(got[:, :, block:], axis=0) + owned_gain * owned_gain
    with jax.named_scope("squares_fsdp"):
        line = [a[None] for a in (gain_master, gain_moment_one, gain_moment_two)]
        line = jnp.concatenate([squares, owned_gain, *line], axis=1)
        line, owned_gain = ordered((line, owned_gain))
        got = to_all(line, n_fsdp, "fsdp")
        lane_squares = jnp.sum(got[:, :, :block], axis=0)
        gain, *gain_states = [got[:, 0, block * i : block * (i + 1)] for i in range(1, 5)]
        ones = jnp.ones((128, 128), jnp.float32)
        total_squares = jnp.dot(lane_squares, ones, precision=lax.Precision.HIGHEST)
    clip_limit = clip_level * math.sqrt(D * HEADS * HEAD + D)
    clip_factor = clip_limit / (jnp.sqrt(total_squares) + 1e-06)
    clip_row = jnp.concatenate([clip_factor] * halves, axis=1)
    zero = jnp.float32(0)
    with jax.named_scope("gain"):
        gain_weights = adamw(*gain_states, gain, clip_factor, 0.0, zero)[0].astype(jnp.bfloat16)
        gain_state = (gain_master, gain_moment_one, gain_moment_two)
        gain_state = [a[None] for a in gain_state]
        gain_state = adamw(*gain_state, owned_gain, clip_factor, 0.0, gain_teacher[None])
        gain_state = jnp.concatenate(gain_state, axis=0)
    with jax.named_scope("weights_fsdp"):
        mine = adamw(*state, own, clip_row, 0.1, zero)[0].astype(jnp.bfloat16)
        mine, gain_weights, gain_state = ordered((mine, gain_weights, gain_state))
        got = to_all(mine, n_fsdp, "fsdp")
    with jax.named_scope("weights_dp"):
        mine = jnp.concatenate([got.reshape(n_fsdp * piece, cols), terms], axis=0)
        got = to_all(mine, n_dp, "dp")
        got = got.reshape(n_dp, n_fsdp + 2, piece, cols)
        state = (master, moment_one, moment_two, teacher)
        weights, gain_weights, *states = finish(got, clip_row, state, gain_weights, gain_state)
        matrix_state, gain_state = states[:4], [a.reshape(block) for a in states[4:]]
    return (
        weights.reshape(rows, cols),
        gain_weights.reshape(rows),
        *matrix_state,
        *gain_state,
    )


def solution(mesh):
    return jax.shard_map(
        shards,
        mesh=mesh,
        in_specs=(
            P("dp", "fsdp", None, "tensor"),
            P("dp", "fsdp", "tensor", None),
            P("fsdp", "tensor"),
            P("fsdp", "tensor"),
            P("fsdp", "tensor"),
            P("fsdp", "tensor"),
            P("fsdp"),
            P("fsdp"),
            P("fsdp"),
            P("fsdp"),
        ),
        out_specs=(
            P(None, "tensor"),
            P(),
            P("fsdp", "tensor"),
            P("fsdp", "tensor"),
            P("fsdp", "tensor"),
            P("fsdp", "tensor"),
            P("fsdp"),
            P("fsdp"),
            P("fsdp"),
            P("fsdp"),
        ),
        check_vma=False,
    )
```

```python
import math

import jax
import jax.numpy as jnp
from jax import lax
from jax.experimental import pallas as pl
from jax.experimental.pallas import tpu as pltpu
from jax.sharding import PartitionSpec as P

D = 2048
HEADS = 8
HEAD = 128
STEP = 20


beta_one = 0.9
beta_two = 0.95
learn_rate = 0.001
teacher_keep = 0.996
clip_level = 2.0
tiny_epsilon = 1e-08


def adamw(parameter, first_moment, second_moment, gradient, clip_factor, weight_decay, shadow):
    scaled = gradient * clip_factor
    first_new = beta_one * first_moment + (1.0 - beta_one) * scaled
    second_new = beta_two * second_moment + (1.0 - beta_two) * scaled * scaled
    corr_one = 1.0 - beta_one**STEP
    corr_two = 1.0 - beta_two**STEP
    direction = first_new / corr_one / (jnp.sqrt(second_new / corr_two) + tiny_epsilon)
    parameter_new = parameter - learn_rate * (direction + weight_decay * parameter)
    shadow_new = teacher_keep * shadow + (1.0 - teacher_keep) * parameter_new
    return (parameter_new, first_new, second_new, shadow_new)


def finish_kernel(*refs):
    got, clip = refs[:2]
    state, gain_weights, gain_state = refs[2:6], refs[6], refs[7]
    weights, gain_out, *outs = refs[8:18]
    new, sems = refs[18:22], refs[22]
    n_dp, pieces, piece, cols = got.shape
    copies = []

    def start(source, target):
        copy = pltpu.make_async_copy(source, target, sems.at[len(copies)])
        copy.start()
        copies.append(copy)

    for d in range(n_dp):
        start(got.at[d, pl.ds(0, pieces - 2)], weights.at[:, d])
    rows = got[:, pieces - 2].astype(jnp.float32) + got[:, pieces - 1].astype(jnp.float32)
    rows = rows.reshape(n_dp * piece, cols)
    values = adamw(*(ref[...] for ref in state[:3]), rows, clip[...], 0.1, state[3][...])
    for i in range(4):
        new[i][...] = values[i]
        start(new[i], outs[i])
    start(gain_weights, gain_out)
    for i in range(4):
        start(gain_state.at[pl.ds(i, 1)], outs[4 + i])
    for copy in copies:
        copy.wait()


def finish(got, clip, state, gain_weights, gain_state):
    n_dp, pieces, piece, cols = got.shape
    owned = jax.ShapeDtypeStruct(state[0].shape, jnp.float32)
    gain = jax.ShapeDtypeStruct((1, gain_state.shape[1]), jnp.float32)
    anywhere = pl.BlockSpec(memory_space=pl.ANY)
    return pl.pallas_call(
        finish_kernel,
        out_shape=[
            jax.ShapeDtypeStruct((pieces - 2, n_dp, piece, cols), jnp.bfloat16),
            jax.ShapeDtypeStruct(gain_weights.shape, jnp.bfloat16),
            *[owned] * 4,
            *[gain] * 4,
        ],
        in_specs=[pl.BlockSpec(memory_space=pltpu.VMEM)] * 8,
        out_specs=[anywhere] * 10,
        scratch_shapes=[
            *[pltpu.VMEM(owned.shape, jnp.float32)] * 4,
            pltpu.SemaphoreType.DMA((9 + n_dp,)),
        ],
        compiler_params=pltpu.CompilerParams(vmem_limit_bytes=8 << 20),
        cost_estimate=pl.CostEstimate(flops=40 * 128 * 256, bytes_accessed=3 << 20, transcendentals=0),
    )(got, clip, *state, gain_weights, gain_state)


def exchange(blocks, axis):
    return lax.all_to_all(blocks, axis, 0, 0, tiled=True)


def to_all(block, count, axis):
    return exchange(jnp.broadcast_to(block[None], (count, *block.shape)), axis)


def shards(
    grad_part,
    gain_grad_part,
    master,
    moment_one,
    moment_two,
    teacher,
    gain_master,
    gain_moment_one,
    gain_moment_two,
    gain_teacher,
):
    n_dp, n_fsdp, n_tensor = (lax.axis_size(a) for a in ("dp", "fsdp", "tensor"))
    rows, cols = grad_part.shape[2:]
    block = rows // n_fsdp
    piece = block // n_dp
    lines = piece * cols // 128
    halves = cols // 128
    ordered = lax.optimization_barrier

    with jax.named_scope("sum_dp"):
        pieces = grad_part.reshape(n_fsdp, n_dp, piece, cols).transpose(1, 0, 2, 3)
        pieces = pieces.reshape(n_dp, n_fsdp * piece, cols)
        pieces, gain_grad_part = ordered((pieces, gain_grad_part))
        gain_part = gain_grad_part.reshape(n_fsdp, 1, block).astype(jnp.float32)
        first, pieces, gain_part = ordered((lax.axis_index("dp") * piece, pieces, gain_part))
        got = exchange(pieces, "dp")
        summed = jnp.sum(got.astype(jnp.float32), axis=0)
    with jax.named_scope("sum_fsdp"):
        part = summed.reshape(n_fsdp, piece, cols)
        part = jnp.concatenate([part[:, :, 128 * h : 128 * (h + 1)] for h in range(halves)], axis=1)
        part = jnp.concatenate([part.reshape(n_fsdp, 1, lines * 128), gain_part], axis=2)
        summed = jnp.sum(exchange(part, "fsdp"), axis=0)
        summed, first = ordered((summed, first))
        own, own_gain = summed[:, : lines * 128].reshape(lines, 128), summed[:, lines * 128 :]
        state = [lax.dynamic_slice_in_dim(a, first, piece) for a in (master, moment_one, moment_two)]
        own_squares = jnp.sum(own * own, axis=0, keepdims=True)
        own = jnp.concatenate([own[piece * h : piece * (h + 1)] for h in range(halves)], axis=1)
        high = lax.reduce_precision(own, 8, 7)
        low = lax.reduce_precision(own - high, 8, 7)
        own = high + low
        terms = jnp.concatenate([high.astype(jnp.bfloat16), low.astype(jnp.bfloat16)], axis=0)
    with jax.named_scope("squares_dp_tensor"):
        line = jnp.concatenate([own_gain, own_squares], axis=1)
        line, own, terms, state = ordered((line, own, terms, state))
        got = to_all(line, n_dp * n_tensor, ("dp", "tensor"))
        got = jnp.sum(got, axis=0)
        owned_gain = got[:, :block]
        squares = got[:, block:] + owned_gain * owned_gain
    with jax.named_scope("squares_fsdp"):
        line = [a[None] for a in (gain_master, gain_moment_one, gain_moment_two)]
        line = jnp.concatenate([squares, owned_gain, *line], axis=1)
        line, owned_gain = ordered((line, owned_gain))
        got = to_all(line, n_fsdp, "fsdp")
        lane_squares = jnp.sum(got[:, :, :block], axis=0)
        gain, *gain_states = [got[:, 0, block * i : block * (i + 1)] for i in range(1, 5)]
        ones = jnp.ones((128, 128), jnp.float32)
        total_squares = jnp.dot(lane_squares, ones, precision=lax.Precision.HIGHEST)
    clip_limit = clip_level * math.sqrt(D * HEADS * HEAD + D)
    clip_factor = clip_limit / (jnp.sqrt(total_squares) + 1e-06)
    clip_row = jnp.concatenate([clip_factor] * halves, axis=1)
    zero = jnp.float32(0)
    with jax.named_scope("gain"):
        gain_weights = adamw(*gain_states, gain, clip_factor, 0.0, zero)[0].astype(jnp.bfloat16)
        gain_state = (gain_master, gain_moment_one, gain_moment_two)
        gain_state = [a[None] for a in gain_state]
        gain_state = adamw(*gain_state, owned_gain, clip_factor, 0.0, gain_teacher[None])
        gain_state = jnp.concatenate(gain_state, axis=0)
    with jax.named_scope("weights_fsdp"):
        mine = adamw(*state, own, clip_row, 0.1, zero)[0].astype(jnp.bfloat16)
        mine, gain_weights, gain_state = ordered((mine, gain_weights, gain_state))
        got = to_all(mine, n_fsdp, "fsdp")
    with jax.named_scope("weights_dp"):
        mine = jnp.concatenate([got.reshape(n_fsdp * piece, cols), terms], axis=0)
        got = to_all(mine, n_dp, "dp")
        got = got.reshape(n_dp, n_fsdp + 2, piece, cols)
        state = (master, moment_one, moment_two, teacher)
        weights, gain_weights, *states = finish(got, clip_row, state, gain_weights, gain_state)
        matrix_state, gain_state = states[:4], [a.reshape(block) for a in states[4:]]
    return (
        weights.reshape(rows, cols),
        gain_weights.reshape(rows),
        *matrix_state,
        *gain_state,
    )


def solution(mesh):
    return jax.shard_map(
        shards,
        mesh=mesh,
        in_specs=(
            P("dp", "fsdp", None, "tensor"),
            P("dp", "fsdp", "tensor", None),
            P("fsdp", "tensor"),
            P("fsdp", "tensor"),
            P("fsdp", "tensor"),
            P("fsdp", "tensor"),
            P("fsdp"),
            P("fsdp"),
            P("fsdp"),
            P("fsdp"),
        ),
        out_specs=(
            P(None, "tensor"),
            P(),
            P("fsdp", "tensor"),
            P("fsdp", "tensor"),
            P("fsdp", "tensor"),
            P("fsdp", "tensor"),
            P("fsdp"),
            P("fsdp"),
            P("fsdp"),
            P("fsdp"),
        ),
        check_vma=False,
    )
```
